128 devices in a mesh: row: 16 (over y, x), col: 8 (over z, core).
Axes of the slice: x: 4, y: 4, z: 4, core: 2. Of those that a mesh axis runs over, the one named last changes fastest.
Arguments:
- spectra: bfloat16 [16384, 4096], P(('row', 'col')), may hold values from 0 to 16, as said below
- projection: bfloat16 [4096, 1024], replicated, may hold values from -0.09375 to 0.09375
- kernel_slot: int32 [16384], P(('row', 'col')), may hold values from 0 to 16383, as said below
- env_image: int32 [16384], P(('row', 'col')), may hold values from 0 to 1023, never falling along the last dimension, each value on 1 to 48 neighbouring positions
- image_atoms: int32 [1024], replicated, may hold values from 8 to 64
Outputs:
- panels: float32 [16384, 1024], P('row')
- trailing: float32 [16384, 16384], P('row', 'col')
The draws below stay inside these ranges and needn't reach their ends.
Inputs may be any that keep to these rules, and one draw needn't show every extreme that they name: `spectra`: Nonnegative. A permutation. With the block of environment e being kernel_slot[e] // 128: among the 128 environments of one device (aligned blocks of 128 in environment order) at most 1 fall in any one block, and in every draw some block receives 1 of them.
All inputs are finite; a program needn't handle non-finite values.
Results may differ from the reference program's by a relative error of at most 0.0063.
Values may be sent and summed in bfloat16 or wider, within the bound.
No kernel may reach another device: no remote copies, remote signals or barrier semaphores. Data moves between devices by JAX's collectives and lax.ppermute only.
A program may use at most 128 MiB of HBM per device.

```python
import math
import jax
import jax.numpy as jnp
import numpy as np
from jax import lax

M = 16384
Q = 4096
K = 1024
NB = 512
PANELS = 2
IMAGES = 1024
MOST = 48
PROW = 16
PCOL = 8
GRID = 128
PER = 128
ROW_GROUP = 1024


def draw_spectra(key, part):
    key_rows, key_cols, key_base = jax.random.split(key, 3)
    row_scale = jnp.exp(jax.random.uniform(key_rows, (M, 1), jnp.float32, 0.0, math.log(10.0)))
    base_values = jax.random.uniform(key_base, (M, Q), jnp.float32)
    col_scale = jnp.exp(jax.random.uniform(key_cols, (1, Q), jnp.float32, math.log(0.1), 0.0))
    return (row_scale * col_scale * base_values).astype(jnp.bfloat16)


def random_ranks(key, shape_rows, shape_cols):
    scores = jax.random.randint(key, (shape_rows, shape_cols), 0, 1 << 20) * shape_cols + jnp.arange(shape_cols, dtype=jnp.int32)[None, :]
    return jnp.argsort(jnp.argsort(scores, axis=1), axis=1).astype(jnp.int32)


def draw_kernel_slot(key, part):
    key_order, key_devices, key_inner = jax.random.split(jax.random.fold_in(key, 7), 3)
    order = random_ranks(key_order, GRID, PER)
    devices_perm = jax.random.permutation(key_devices, GRID).astype(jnp.int32)
    values = order * GRID + devices_perm[:, None]
    blocks = values // PER
    shuffle = random_ranks(key_inner, GRID, PER)
    inner = shuffle[blocks, values % PER]
    return (blocks * PER + inner).reshape(-1).astype(jnp.int32)


def place_ends(result, stream_key, low, high):
    shape = result.shape
    spot = [jax.random.randint(jax.random.fold_in(stream_key, axis), (), 0, shape[axis]) for axis in range(len(shape))]
    result = result.at[tuple(spot)].set(low)
    longest = shape.index(max(shape))
    spot[longest] = (spot[longest] + 1) % shape[longest]
    return result.at[tuple(spot)].set(high)


def length_profile(amount, total, most, skew):
    weights = [(1 << 20) // math.isqrt(grade ** skew) + 1 for grade in range(2, amount + 1)]
    surplus, given = total - most - (amount - 1), [1] * (amount - 1)
    while surplus > 0:
        candidates = [i for i in range(amount - 1) if given[i] < most]
        whole, remaining = sum([weights[i] for i in candidates]), surplus
        for i in candidates:
            addition = min(most - given[i], max(1, remaining * weights[i] // whole), surplus)
            given[i] = given[i] + addition
            surplus = surplus - addition
    return np.array([most] + given)


def uneven(rng, amount, total, bound, skew):
    if amount == 2:
        one = jax.random.randint(rng, (), max(1, total - bound), min(bound, total - 1) + 1)
        return jnp.stack([one, total - one])
    tallies = jnp.asarray(length_profile(amount, total, bound, skew), jnp.int32)
    pairs = (amount - 1) // 2
    giver, sink = tallies[1:1 + 2 * pairs:2], tallies[2:2 + 2 * pairs:2]
    margin = jnp.minimum(giver - 1, bound - sink)
    passed = jax.random.randint(jax.random.fold_in(rng, 1), (pairs,), 0, 1 << 20) % (margin + 1)
    tallies = tallies.at[1:1 + 2 * pairs:2].set(giver - passed).at[2:2 + 2 * pairs:2].set(sink + passed)
    return tallies[jax.random.permutation(jax.random.fold_in(rng, 2), amount)]


def normal_values(stream_key, shape, width, reach, held_as=jnp.bfloat16):
    return jnp.clip(width * jax.random.normal(stream_key, shape, jnp.float32), -reach, reach).astype(held_as)


def setup_inputs(seed: int = 0) -> dict:
    keys = jax.random.split(jax.random.key(seed), 6)
    spectra = draw_spectra(jax.random.fold_in(keys[5], 71), 0)
    projection = normal_values(keys[1], (Q, K), Q ** -0.5, 0.09375)
    kernel_slot = draw_kernel_slot(jax.random.fold_in(keys[5], 71), 0)
    env_image = jnp.searchsorted(jnp.cumsum(uneven(keys[3], IMAGES, M, MOST, 2)), jnp.arange(M), side="right").astype(jnp.int32)
    image_atoms = place_ends(jax.random.randint(keys[4], (IMAGES,), 8, 65), jax.random.fold_in(keys[4], 1), 8, 64).astype(jnp.int32)
    return dict(spectra=spectra, projection=projection, kernel_slot=kernel_slot, env_image=env_image, image_atoms=image_atoms)


ATOM_RIDGE = 0.02
NORM_EPS = 1e-06

def reference(spectra, projection, kernel_slot, env_image, image_atoms):
    projected = jnp.dot(spectra.astype(jnp.float32), projection.astype(jnp.float32), preferred_element_type=jnp.float32)
    factor = lax.rsqrt(lax.optimization_barrier(jnp.mean(projected * projected, axis=1, keepdims=True)) + NORM_EPS) * K ** (-0.5)
    unit_rows = (projected * factor).astype(jnp.bfloat16)
    stored = jnp.zeros((M, K), jnp.bfloat16).at[kernel_slot].set(unit_rows)
    ridge_env = ATOM_RIDGE * jnp.take(image_atoms, env_image).astype(jnp.float32)
    ridge_diag = jnp.zeros((M,), jnp.float32).at[kernel_slot].set(ridge_env)
    gram_matrix = jnp.dot(stored.astype(jnp.float32), stored.T.astype(jnp.float32), preferred_element_type=jnp.float32)
    positions = jnp.arange(M, dtype=jnp.int32)
    covariance = (gram_matrix * gram_matrix).at[positions, positions].add(ridge_diag)
    tile_of = positions % ROW_GROUP // NB * PROW + positions // ROW_GROUP
    panel_list = []
    for panel_index in range(PANELS):
        pivot_start = panel_index % PROW * ROW_GROUP + panel_index // PROW * NB
        lower_factor = jnp.linalg.cholesky(covariance[pivot_start:pivot_start + NB, pivot_start:pivot_start + NB])
        solved = lax.linalg.triangular_solve(lower_factor, covariance[:, pivot_start:pivot_start + NB], left_side=False, lower=True, transpose_a=True)
        solved = jnp.where((tile_of >= panel_index)[:, None], solved, 0.0)
        covariance = covariance - jnp.dot(solved.astype(jnp.float32), solved.T.astype(jnp.float32), precision=lax.Precision.HIGHEST, preferred_element_type=jnp.float32)
        panel_list.append(solved)
    panels = jnp.concatenate(panel_list, axis=1)
    trailing = covariance.reshape(M, PROW // PCOL, PCOL, ROW_GROUP).transpose(0, 2, 1, 3).reshape(M, M)
    return (panels, trailing)
```

```python
import functools

import jax
import jax.numpy as jnp
from jax import lax
from jax.experimental import pallas as pl
from jax.experimental.pallas import tpu as pltpu
from jax.sharding import PartitionSpec as P

NB = 512
PANELS = 2
ATOM_RIDGE = 0.02
NORM_EPS = 1e-06
EXTRA = 128
BLOCK = 128
NN = ((1,), (0,))
NT = ((1,), (1,))


def split(a):
    high = a.astype(jnp.bfloat16)
    return high, (a - high.astype(jnp.float32)).astype(jnp.bfloat16)


def halves(a):
    high = lax.reduce_precision(a, 8, 7)
    return high.astype(jnp.bfloat16), (a - high).astype(jnp.bfloat16)


def dot(a, b, dims):
    return lax.dot_general(a, b, (dims, ((), ())), preferred_element_type=jnp.float32)


def dot3(a, b, dims):
    a_high, a_low = a
    b_high, b_low = b
    return dot(a_high, b_high, dims) + (dot(a_high, b_low, dims) + dot(a_low, b_high, dims))


def eliminate(rows, lane, sub):
    mat = list(rows)
    count = len(mat)
    inv = [jnp.where(lane == sub + 8 * i, 1.0, 0.0).astype(jnp.float32) for i in range(count)]
    out = [None] * count

    def wide(value):
        return jnp.broadcast_to(value, (8, BLOCK))

    for j in range(0, 8 * count, 2):
        v, s = j // 8, j % 8
        row0, row1 = wide(mat[v][s : s + 1, :]), wide(mat[v][s + 1 : s + 2, :])
        inv0, inv1 = wide(inv[v][s : s + 1, :]), wide(inv[v][s + 1 : s + 2, :])
        a, b, c = wide(row0[:, j : j + 1]), wide(row0[:, j + 1 : j + 2]), wide(row1[:, j + 1 : j + 2])
        det = a * c - b * b
        r = 1.0 / det
        p0, p1 = (c * row0 - b * row1) * r, (a * row1 - b * row0) * r
        q0, q1 = (c * inv0 - b * inv1) * r, (a * inv1 - b * inv0) * r
        ra, rd = lax.rsqrt(a), lax.rsqrt(det)
        done0, done1 = inv0 * ra, (a * inv1 - b * inv0) * (ra * rd)
        before = inv[v] if out[v] is None else out[v]
        out[v] = jnp.where(sub == s, done0, jnp.where(sub == s + 1, done1, before))
        for i in range(v, count):
            if i == v and s == 6:
                continue
            c0, c1 = wide(mat[i][:, j : j + 1]), wide(mat[i][:, j + 1 : j + 2])
            if i == v:
                keep = sub > s + 1
                c0, c1 = jnp.where(keep, c0, 0.0), jnp.where(keep, c1, 0.0)
            mat[i] = mat[i] - (c0 * p0 + c1 * p1)
            inv[i] = inv[i] - (c0 * q0 + c1 * q1)
    return out


def inverse_factor_kernel(n, a_ref, x_ref, w_ref, d_ref):
    lane = lax.broadcasted_iota(jnp.int32, (8, BLOCK), 1)
    sub = lax.broadcasted_iota(jnp.int32, (8, BLOCK), 0)
    w_ref[:, :n] = a_ref[...]
    diagonal = lax.broadcasted_iota(jnp.int32, (n, n), 0) == lax.broadcasted_iota(jnp.int32, (n, n), 1)
    w_ref[:, n:] = jnp.where(diagonal, 1.0, 0.0)

    def step(k, carry):
        at = pl.multiple_of(k * BLOCK, BLOCK)
        corner = w_ref[pl.ds(at, BLOCK), pl.ds(at, BLOCK)]
        rows = eliminate([corner[8 * i : 8 * i + 8, :] for i in range(BLOCK // 8)], lane, sub)
        for i in range(BLOCK // 8):
            d_ref[8 * i : 8 * i + 8, :] = rows[i]
        inv = split(d_ref[...])
        upper = dot3(inv, split(w_ref[pl.ds(at, BLOCK), :]), NN)
        x_ref[pl.ds(at, BLOCK), :] = upper[:, n:]
        upper = split(upper)

        def update(i, carry):
            here = pl.multiple_of(i * BLOCK, BLOCK)
            lower = dot3(split(w_ref[pl.ds(here, BLOCK), pl.ds(at, BLOCK)]), inv, NT)
            w_ref[pl.ds(here, BLOCK), :] = w_ref[pl.ds(here, BLOCK), :] - dot3(split(lower), upper, NN)
            return carry

        lax.fori_loop(k + 1, n // BLOCK, update, 0)
        return carry

    lax.fori_loop(0, n // BLOCK, step, 0)


def inverse_factor(a):
    n = a.shape[0]
    return pl.pallas_call(
        functools.partial(inverse_factor_kernel, n),
        out_shape=jax.ShapeDtypeStruct((n, n), jnp.float32),
        in_specs=[pl.BlockSpec(memory_space=pltpu.VMEM)],
        out_specs=pl.BlockSpec(memory_space=pltpu.VMEM),
        scratch_shapes=[pltpu.VMEM((n, 2 * n), jnp.float32), pltpu.VMEM((BLOCK, BLOCK), jnp.float32)],
        compiler_params=pltpu.CompilerParams(vmem_limit_bytes=40 << 20),
        name="inverse_factor",
    )(a)


def in_block_order(rows):
    place = rows[:, -EXTRA].astype(jnp.int32)
    pick = lax.broadcasted_iota(jnp.int32, (rows.shape[0], rows.shape[0]), 0) == place[None, :]
    return dot(pick.astype(jnp.bfloat16), rows, NN).astype(jnp.bfloat16)


def body(spectra, projection, kernel_slot, env_image, image_atoms):
    grid_rows = lax.axis_size("row")
    grid_cols = lax.axis_size("col")
    devices = grid_rows * grid_cols
    per_device = spectra.shape[0]
    total_rows = per_device * devices
    width = projection.shape[1]
    row_group = total_rows // grid_rows
    col_group = total_rows // grid_cols
    row_index = lax.axis_index("row")
    col_index = lax.axis_index("col")
    projected = jnp.dot(spectra, projection, preferred_element_type=jnp.float32)
    factor = lax.rsqrt(
        jnp.mean(projected * projected, axis=1, keepdims=True) + NORM_EPS
    ) * width ** (-0.5)
    unit_rows = (projected * factor).astype(jnp.bfloat16)

    images = jnp.arange(image_atoms.shape[0], dtype=jnp.int32)
    atoms = jnp.sum(jnp.where(env_image[:, None] == images[None, :], image_atoms[None, :], 0), axis=1)
    extra_lane = jnp.arange(EXTRA, dtype=jnp.int32)[None, :]
    extra = jnp.where(extra_lane == 0, (kernel_slot % per_device)[:, None], atoms[:, None])
    packed = jnp.concatenate([unit_rows, extra.astype(jnp.bfloat16)], axis=1)

    block = kernel_slot // per_device
    blocks = jnp.arange(devices, dtype=jnp.int32)
    by_block = dot((blocks[:, None] == block[None, :]).astype(jnp.bfloat16), packed, NN).astype(jnp.bfloat16)
    dest_row, dest_col = blocks // grid_cols, blocks % grid_cols
    turned_block = (dest_col + grid_cols * (dest_row // grid_cols)) * grid_cols + dest_row % grid_cols
    by_turned = dot((turned_block[:, None] == block[None, :]).astype(jnp.bfloat16), packed, NN).astype(jnp.bfloat16)

    tile_blocks = NB // per_device
    group_blocks = row_group // per_device
    pivot_rows = []
    for panel_index in range(PANELS):
        first = panel_index % grid_rows * group_blocks + panel_index // grid_rows * tile_blocks
        pivot_rows.append(by_block[first : first + tile_blocks])
    pivot_rows = jnp.concatenate(pivot_rows, axis=0)
    pivot_blocks = pivot_rows.shape[0]
    spread = jnp.broadcast_to(pivot_rows[None], (devices,) + pivot_rows.shape)

    both = ("row", "col")
    pivots = lax.all_to_all(spread, both, split_axis=0, concat_axis=0, tiled=True)
    turned = lax.all_to_all(by_turned, both, split_axis=0, concat_axis=0, tiled=True)
    own = lax.all_to_all(by_block, both, split_axis=0, concat_axis=0, tiled=True)
    col_rows = lax.all_gather(in_block_order(turned)[:, :width], "row", axis=0, tiled=True)
    row_rows = lax.all_gather(in_block_order(own), "col", axis=0, tiled=True)

    pivots = jnp.concatenate([in_block_order(pivots[:, i]) for i in range(pivot_blocks)], axis=0)
    order = pivots.shape[0]
    pivot_ridge = ATOM_RIDGE * pivots[:, -1].astype(jnp.float32)
    pivots = pivots[:, :width]
    pivot_gram = dot(pivots, pivots, NT)
    diagonal = jnp.arange(order)[:, None] == jnp.arange(order)[None, :]
    inverse = inverse_factor(pivot_gram * pivot_gram + jnp.where(diagonal, pivot_ridge[:, None], 0.0))

    ridge = ATOM_RIDGE * row_rows[:, -1].astype(jnp.float32)
    row_rows = row_rows[:, :width]
    positions = jnp.arange(row_group, dtype=jnp.int32)
    row_tile = positions // NB * grid_rows + row_index
    pivot_of = jnp.arange(order, dtype=jnp.int32)
    pivot_stored = pivot_of // NB % grid_rows * row_group + pivot_of // NB // grid_rows * NB + pivot_of % NB
    stored = row_index * row_group + positions
    row_gram = dot(row_rows, pivots, NT)
    row_cov = row_gram * row_gram + jnp.where(stored[:, None] == pivot_stored[None, :], ridge[:, None], 0.0)
    inverse_parts = halves(inverse)
    panels = dot3(halves(row_cov), inverse_parts, NT)
    panels = jnp.where(row_tile[:, None] >= pivot_of[None, :] // NB, panels, 0.0)
    weights = dot3(halves(panels), inverse_parts, NN)

    col_gram = dot(pivots, col_rows, NT)
    groups = jnp.arange(col_group, dtype=jnp.int32) // row_group * grid_cols + col_index
    col_stored = groups * row_group + jnp.arange(col_group, dtype=jnp.int32) % row_group
    col_hit = pivot_stored[:, None] == col_stored[None, :]
    col_cov = col_gram * col_gram + jnp.where(col_hit, pivot_ridge[:, None], 0.0)
    gram = dot(row_rows, col_rows, NT)
    covariance = gram * gram + jnp.where(stored[:, None] == col_stored[None, :], ridge[:, None], 0.0)
    trailing = covariance - dot3(halves(weights), halves(col_cov), NN)
    return panels, trailing


def solution(mesh):
    in_specs = (P(("row", "col"), None), P(), P(("row", "col")), P(("row", "col")), P())
    out_specs = (P("row", None), P("row", "col"))
    return jax.shard_map(body, mesh=mesh, in_specs=in_specs, out_specs=out_specs, check_vma=False)
```

```python
import functools

import jax
import jax.numpy as jnp
from jax import lax
from jax.experimental import pallas as pl
from jax.experimental.pallas import tpu as pltpu
from jax.sharding import PartitionSpec as P

NB = 512
PANELS = 2
ATOM_RIDGE = 0.02
NORM_EPS = 1e-06
EXTRA = 128
PIVOT_ATOMS = 1
OWN_ATOMS = 4
BLOCK = 128
NN = ((1,), (0,))
NT = ((1,), (1,))


def split(a):
    high = a.astype(jnp.bfloat16)
    return high, (a - high.astype(jnp.float32)).astype(jnp.bfloat16)


def halves(a):
    high = lax.reduce_precision(a, 8, 7)
    return high.astype(jnp.bfloat16), (a - high).astype(jnp.bfloat16)


def dot(a, b, dims):
    return lax.dot_general(a, b, (dims, ((), ())), preferred_element_type=jnp.float32)


def dot3(a, b, dims):
    a_high, a_low = a
    b_high, b_low = b
    return dot(a_high, b_high, dims) + (dot(a_high, b_low, dims) + dot(a_low, b_high, dims))


def eliminate(mat_ref, inv_ref, out_ref):
    sub = lax.broadcasted_iota(jnp.int32, (8, BLOCK), 0)
    column = lax.broadcasted_iota(jnp.int32, (8, BLOCK), 1)
    count = BLOCK // 8

    def wide(value):
        return jnp.broadcast_to(value, (8, BLOCK))

    for v in range(count):
        inv_ref[8 * v : 8 * v + 8, :] = jnp.where(column == sub + 8 * v, 1.0, 0.0)
    for v in range(count):
        mat, inv = mat_ref[8 * v : 8 * v + 8, :], inv_ref[8 * v : 8 * v + 8, :]
        cols = [wide(mat[:, 8 * v + k : 8 * v + k + 1]) for k in range(8)]
        done = inv
        for s in range(0, 8, 2):
            c0, c1 = cols[s], cols[s + 1]
            a, b, c = wide(c0[s : s + 1]), wide(c0[s + 1 : s + 2]), wide(c1[s + 1 : s + 2])
            det = a * c - b * b
            r = 1.0 / det
            ar, br, cr = a * r, b * r, c * r
            u, w = c0 * cr - c1 * br, c1 * ar - c0 * br
            u = jnp.where(sub == s, 1.0 - cr, jnp.where(sub == s + 1, br, u))
            w = jnp.where(sub == s, br, jnp.where(sub == s + 1, 1.0 - ar, w))

            def apply(x):
                return x - (u * wide(x[s : s + 1]) + w * wide(x[s + 1 : s + 2]))

            for k in range(s + 2, 8):
                cols[k] = apply(cols[k])
            i0, i1 = wide(inv[s : s + 1]), wide(inv[s + 1 : s + 2])
            ra = lax.rsqrt(a)
            done = jnp.where(sub == s, i0 * ra, jnp.where(sub == s + 1, (a * i1 - b * i0) * (ra * lax.rsqrt(det)), done))
            mat, inv = apply(mat), apply(inv)
        out_ref[8 * v : 8 * v + 8, :] = done
        mats = [wide(mat[k : k + 1]) for k in range(8)]
        invs = [wide(inv[k : k + 1]) for k in range(8)]
        for i in range(v + 1, count):
            at = slice(8 * i, 8 * i + 8)
            x = mat_ref[at, :]
            parts = [wide(x[:, 8 * v + k : 8 * v + k + 1]) for k in range(8)]
            mat_ref[at, :] = x - tree_sum([p * m for p, m in zip(parts, mats)])
            inv_ref[at, :] = inv_ref[at, :] - tree_sum([p * m for p, m in zip(parts, invs)])


def tree_sum(values):
    while len(values) > 1:
        values = [values[i] + values[i + 1] for i in range(0, len(values), 2)]
    return values[0]


def pivot_kernel(n, width, raw_ref, rows_ref, high_ref, low_ref, sorted_ref, w_ref, mat_ref, inv_ref, out_ref):
    k = pl.program_id(0)
    count = n // BLOCK

    @pl.when(k == 0)
    def _():
        raw = raw_ref[:, : width + EXTRA]
        pick = (lax.broadcasted_iota(jnp.int32, (8, EXTRA), 1) == 0).astype(jnp.bfloat16)
        place = dot(pick, raw[:, width:], NT)[0:1, :].astype(jnp.int32)
        target = lax.broadcasted_iota(jnp.int32, (1, n), 1) % count * BLOCK + place
        chosen = jnp.where(lax.broadcasted_iota(jnp.int32, (n, n), 0) == target, 1.0, 0.0).astype(jnp.bfloat16)
        sorted_ref[...] = dot(chosen, raw, NN).astype(jnp.bfloat16)
        gram = dot(sorted_ref[:, :width], sorted_ref[:, :width], NT)
        ridge = ATOM_RIDGE * sorted_ref[:, lane(width, PIVOT_ATOMS)].astype(jnp.float32)
        hit = lax.broadcasted_iota(jnp.int32, (n, n), 0) == lax.broadcasted_iota(jnp.int32, (n, n), 1)
        w_ref[...] = gram * gram + jnp.where(hit, ridge, 0.0)

    at = pl.multiple_of(k * BLOCK, BLOCK)
    rows_ref[...] = sorted_ref[pl.ds(at, BLOCK), :]
    mat_ref[...] = w_ref[pl.ds(at, BLOCK), pl.ds(at, BLOCK)]
    eliminate(mat_ref, inv_ref, out_ref)

    for step in range(count):

        @pl.when(k == step)
        def _(step=step):
            here, after = slice(step * BLOCK, (step + 1) * BLOCK), slice((step + 1) * BLOCK, n)
            inv = split(out_ref[...])
            high_ref[:, here], low_ref[:, here] = inv
            if step:
                left = split(dot3(inv, split(w_ref[here, : step * BLOCK]), NN))
                high_ref[:, : step * BLOCK], low_ref[:, : step * BLOCK] = left
            if step + 1 < count:
                zeros = jnp.zeros((BLOCK, n - (step + 1) * BLOCK), jnp.bfloat16)
                high_ref[:, after], low_ref[:, after] = zeros, zeros
                right = split(dot3(inv, split(w_ref[here, after]), NN))
                lower = split(dot3(split(w_ref[after, here]), inv, NT))
                w_ref[after, after] = w_ref[after, after] - dot3(lower, right, NN)
                w_ref[after, here] = -dot3(lower, inv, NN)
                if step:
                    w_ref[after, : step * BLOCK] = w_ref[after, : step * BLOCK] - dot3(lower, left, NN)


def lane(width, index):
    return slice(width + index, width + index + 1)


def pivot_factor(raw, width):
    n, packed = raw.shape[0], width + EXTRA
    return pl.pallas_call(
        functools.partial(pivot_kernel, n, width),
        grid=(n // BLOCK,),
        out_shape=tuple(pltpu.HBM((n, size), jnp.bfloat16) for size in (packed, n, n)),
        in_specs=[pl.BlockSpec(raw.shape, lambda k: (0, 0), pipeline_mode=pl.Buffered(1))],
        out_specs=tuple(pl.BlockSpec((BLOCK, size), lambda k: (k, 0)) for size in (packed, n, n)),
        scratch_shapes=[pltpu.VMEM((n, packed), jnp.bfloat16), pltpu.VMEM((n, n), jnp.float32)]
        + [pltpu.VMEM((BLOCK, BLOCK), jnp.float32)] * 3,
        compiler_params=pltpu.CompilerParams(vmem_limit_bytes=40 << 20),
        name="pivot_factor",
    )(pltpu.with_memory_space_constraint(raw, pltpu.HBM))


def pivot_stored(index, grid_rows, row_group):
    panel = index // NB
    return panel % grid_rows * row_group + panel // grid_rows * NB + index % NB


def final_kernel(
    grid_rows, grid_cols, row_group, width, row_tiles,
    at_ref, rows_ref, pivots_ref, high_ref, low_ref, col_ref, panel_ref, out_ref, wh_ref, wl_ref, ch_ref, cl_ref,
):
    step = pl.program_id(0)
    n = pivots_ref.shape[0]

    @pl.when(step < row_tiles)
    def _():
        tile = panel_ref.shape[0]
        at = pl.ds(pl.multiple_of(step * tile, tile), tile)
        gram = dot(rows_ref[at, :width], pivots_ref[:, :width], NT)
        ridge = ATOM_RIDGE * rows_ref[at, lane(width, OWN_ATOMS)].astype(jnp.float32)
        local = lax.broadcasted_iota(jnp.int32, (tile, n), 0) + step * tile
        pivot = lax.broadcasted_iota(jnp.int32, (tile, n), 1)
        stored = local + at_ref[0] * row_group
        cov = split(gram * gram + jnp.where(stored == pivot_stored(pivot, grid_rows, row_group), ridge, 0.0))
        row_tile = local // NB * grid_rows + at_ref[0]
        parts = []
        for p in range(n // NB):
            here, upto = slice(p * NB, (p + 1) * NB), slice(0, (p + 1) * NB)
            part = dot3([x[:, upto] for x in cov], (high_ref[here, upto], low_ref[here, upto]), NT)
            part = jnp.where(row_tile[:, here] >= p, part, 0.0)
            panel_ref[:, here] = part
            parts.append(split(part))
        panel = [jnp.concatenate([x[i] for x in parts], axis=1) for i in range(2)]
        for p in range(n // NB):
            here, since = slice(p * NB, (p + 1) * NB), slice(p * NB, n)
            part = dot3([x[:, since] for x in panel], (high_ref[since, here], low_ref[since, here]), NN)
            wh_ref[at, here], wl_ref[at, here] = split(part)

    @pl.when(step >= row_tiles)
    def _():
        total, tile = out_ref.shape
        col = lax.broadcasted_iota(jnp.int32, (n, tile), 1) + (step - row_tiles) * tile
        col_stored = (col // row_group * grid_cols + at_ref[1]) * row_group + col % row_group
        row = lax.broadcasted_iota(jnp.int32, (n, tile), 0)
        gram = dot(pivots_ref[:, :width], col_ref[...], NT)
        ridge = ATOM_RIDGE * pivots_ref[:, lane(width, PIVOT_ATOMS)].astype(jnp.float32)
        hit = pivot_stored(row, grid_rows, row_group) == col_stored
        ch_ref[...], cl_ref[...] = split(gram * gram + jnp.where(hit, ridge, 0.0))
        gram = dot(rows_ref[:, :width], col_ref[...], NT)
        ridge = ATOM_RIDGE * rows_ref[:, lane(width, OWN_ATOMS)].astype(jnp.float32)
        hit = row[:total] + at_ref[0] * row_group == col_stored[:total]
        update = dot3((wh_ref[...], wl_ref[...]), (ch_ref[...], cl_ref[...]), NN)
        out_ref[...] = gram * gram + jnp.where(hit, ridge, 0.0) - update


def final(at, rows, pivots, high, low, cols, grid_rows, grid_cols, row_group, width, row_tile=512, col_tile=256):
    count, total, n = rows.shape[0], cols.shape[0], pivots.shape[0]
    row_tiles = count // row_tile
    whole = lambda x: pl.BlockSpec(x.shape, lambda i, at: (0, 0), pipeline_mode=pl.Buffered(1))
    return pl.pallas_call(
        functools.partial(final_kernel, grid_rows, grid_cols, row_group, width, row_tiles),
        grid_spec=pltpu.PrefetchScalarGridSpec(
            num_scalar_prefetch=1,
            grid=(row_tiles + total // col_tile,),
            in_specs=[whole(rows), whole(pivots), whole(high), whole(low)]
            + [pl.BlockSpec((col_tile, width), lambda i, at: (jnp.maximum(i - row_tiles, 0), 0))],
            out_specs=(
                pl.BlockSpec((row_tile, n), lambda i, at: (jnp.minimum(i, row_tiles - 1), 0)),
                pl.BlockSpec((count, col_tile), lambda i, at: (0, jnp.maximum(i - row_tiles, 0))),
            ),
            scratch_shapes=[pltpu.VMEM((count, n), jnp.bfloat16)] * 2 + [pltpu.VMEM((n, col_tile), jnp.bfloat16)] * 2,
        ),
        out_shape=(
            jax.ShapeDtypeStruct((count, n), jnp.float32),
            jax.ShapeDtypeStruct((count, total), jnp.float32),
        ),
        compiler_params=pltpu.CompilerParams(vmem_limit_bytes=52 << 20),
        name="final",
    )(at, pltpu.with_memory_space_constraint(rows, pltpu.HBM), pivots, high, low, cols)


def in_block_order(rows, place):
    pick = lax.broadcasted_iota(jnp.int32, (rows.shape[0], rows.shape[0]), 0) == place.astype(jnp.int32)[None, :]
    return dot(pick.astype(jnp.bfloat16), rows, NN).astype(jnp.bfloat16)


def body(spectra, projection, kernel_slot, env_image, image_atoms):
    grid_rows = lax.axis_size("row")
    grid_cols = lax.axis_size("col")
    devices = grid_rows * grid_cols
    per_device = spectra.shape[0]
    width = projection.shape[1]
    row_group = per_device * grid_cols
    both = ("row", "col")
    projected = jnp.dot(spectra, projection, preferred_element_type=jnp.float32)
    factor = lax.rsqrt(
        jnp.mean(projected * projected, axis=1, keepdims=True) + NORM_EPS
    ) * width ** (-0.5)
    unit_rows = (projected * factor).astype(jnp.bfloat16)

    images = jnp.arange(image_atoms.shape[0], dtype=jnp.int32)
    atoms = jnp.sum(jnp.where(env_image[:, None] == images[None, :], image_atoms[None, :], 0), axis=1)
    extra_lane = jnp.arange(EXTRA, dtype=jnp.int32)[None, :]
    extra = jnp.where(extra_lane == 0, (kernel_slot % per_device)[:, None], atoms[:, None])
    packed = jnp.concatenate([unit_rows, extra.astype(jnp.bfloat16)], axis=1)

    block = kernel_slot // per_device
    blocks = jnp.arange(devices, dtype=jnp.int32)
    tile_blocks = NB // per_device
    group_blocks = row_group // per_device
    pivot_block = []
    for panel_index in range(PANELS):
        first = panel_index % grid_rows * group_blocks + panel_index // grid_rows * tile_blocks
        pivot_block += [first + i for i in range(tile_blocks)]
    pivot_block = jnp.stack([jnp.int32(i) for i in pivot_block])
    pivot_rows = dot((pivot_block[:, None] == block[None, :]).astype(jnp.bfloat16), packed, NN).astype(jnp.bfloat16)
    count = pivot_rows.shape[0]
    dest_row, dest_col = blocks // grid_cols, blocks % grid_cols
    turned_block = (dest_col + grid_cols * (dest_row // grid_cols)) * grid_cols + dest_row % grid_cols
    turned = dot((turned_block[:, None] == block[None, :]).astype(jnp.bfloat16), packed, NN).astype(jnp.bfloat16)
    own = dot((blocks[:, None] == block[None, :]).astype(jnp.bfloat16), packed, NN).astype(jnp.bfloat16)
    pair = jnp.concatenate([turned[:, :width], own[:, :width]], axis=1).reshape(devices, count, -1)
    spare = jnp.arange(EXTRA)
    spare = jnp.where(spare == 2, turned[:, width, None], jnp.where(spare == 3, own[:, width, None], own[:, width + 1, None]))
    head = jnp.broadcast_to(pivot_rows[None, :, :width], (devices, count, width))
    middle = jnp.where(jnp.arange(EXTRA) < 2, pivot_rows[None, :, width:], spare[:, None, :])
    parcel = jnp.concatenate([head, middle, pair], axis=2)

    parcel = lax.all_to_all(parcel, both, split_axis=0, concat_axis=0, tiled=True)
    pair = parcel[:, :, width + EXTRA :].reshape(per_device, 2 * width)
    places = parcel[:, 0, width : width + EXTRA]
    turned = in_block_order(pair[:, :width], places[:, 2])
    own = in_block_order(jnp.concatenate([pair[:, width:], places], axis=1), places[:, 3])
    col_rows = lax.all_gather(turned, "row", axis=0, tiled=True)
    row_rows = jnp.broadcast_to(own[None], (grid_cols,) + own.shape)
    row_rows = lax.all_to_all(row_rows, "col", split_axis=0, concat_axis=0)
    row_rows = row_rows.reshape(row_group, -1)
    pivots, high, low = pivot_factor(parcel.reshape(-1, parcel.shape[-1]), width)

    at = jnp.stack([lax.axis_index("row"), lax.axis_index("col")]).astype(jnp.int32)
    return final(at, row_rows, pivots, high, low, col_rows, grid_rows, grid_cols, row_group, width)


def solution(mesh):
    in_specs = (P(("row", "col"), None), P(), P(("row", "col")), P(("row", "col")), P())
    out_specs = (P("row", None), P("row", "col"))
    return jax.shard_map(body, mesh=mesh, in_specs=in_specs, out_specs=out_specs, check_vma=False)
```

```python
import functools

import jax
import jax.numpy as jnp
from jax import lax
from jax.experimental import pallas as pl
from jax.experimental.pallas import tpu as pltpu
from jax.sharding import PartitionSpec as P

NB = 512
PANELS = 2
ATOM_RIDGE = 0.02
NORM_EPS = 1e-06
EXTRA = 128
PIVOT_ATOMS = 1
OWN_ATOMS = 4
BLOCK = 128
PIECE = 256
NN = ((1,), (0,))
NT = ((1,), (1,))


def split(a):
    high = a.astype(jnp.bfloat16)
    return high, (a - high.astype(jnp.float32)).astype(jnp.bfloat16)


def halves(a):
    high = lax.reduce_precision(a, 8, 7)
    return high.astype(jnp.bfloat16), (a - high).astype(jnp.bfloat16)


def dot(a, b, dims):
    return lax.dot_general(a, b, (dims, ((), ())), preferred_element_type=jnp.float32)


def dot3(a, b, dims):
    a_high, a_low = a
    b_high, b_low = b
    return dot(a_high, b_high, dims) + (dot(a_high, b_low, dims) + dot(a_low, b_high, dims))


def eliminate(mat_ref, inv_ref, out_ref):
    sub = lax.broadcasted_iota(jnp.int32, (8, BLOCK), 0)
    column = lax.broadcasted_iota(jnp.int32, (8, BLOCK), 1)
    count = BLOCK // 8

    def wide(value):
        return jnp.broadcast_to(value, (8, BLOCK))

    for v in range(count):
        inv_ref[8 * v : 8 * v + 8, :] = jnp.where(column == sub + 8 * v, 1.0, 0.0)
    for v in range(count):
        mat, inv = mat_ref[8 * v : 8 * v + 8, :], inv_ref[8 * v : 8 * v + 8, :]
        cols = [wide(mat[:, 8 * v + k : 8 * v + k + 1]) for k in range(8)]
        done = inv
        for s in range(0, 8, 2):
            c0, c1 = cols[s], cols[s + 1]
            a, b, c = wide(c0[s : s + 1]), wide(c0[s + 1 : s + 2]), wide(c1[s + 1 : s + 2])
            det = a * c - b * b
            r = 1.0 / det
            c0, c1 = c0 - jnp.where(sub == s, 1.0, 0.0), c1 - jnp.where(sub == s + 1, 1.0, 0.0)
            u, w = c0 * c - c1 * b, c1 * a - c0 * b

            def apply(x):
                return x - (u * wide(x[s : s + 1]) + w * wide(x[s + 1 : s + 2])) * r

            for k in range(s + 2, 8):
                cols[k] = apply(cols[k])
            i0, i1 = wide(inv[s : s + 1]), wide(inv[s + 1 : s + 2])
            ra = lax.rsqrt(a)
            done = jnp.where(sub == s, i0 * ra, jnp.where(sub == s + 1, (a * i1 - b * i0) * (ra * lax.rsqrt(det)), done))
            mat, inv = apply(mat), apply(inv)
        out_ref[8 * v : 8 * v + 8, :] = done
        mats = [wide(mat[k : k + 1]) for k in range(8)]
        invs = [wide(inv[k : k + 1]) for k in range(8)]
        for i in range(v + 1, count):
            at = slice(8 * i, 8 * i + 8)
            x = mat_ref[at, :]
            parts = [wide(x[:, 8 * v + k : 8 * v + k + 1]) for k in range(8)]
            mat_ref[at, :] = x - tree_sum([p * m for p, m in zip(parts, mats)])
            inv_ref[at, :] = inv_ref[at, :] - tree_sum([p * m for p, m in zip(parts, invs)])


def tree_sum(values):
    while len(values) > 1:
        values = [values[i] + values[i + 1] for i in range(0, len(values), 2)]
    return values[0]


def pivot_kernel(n, width, raw_ref, rows_ref, high_ref, low_ref, sorted_ref, w_ref, mat_ref, inv_ref, out_ref):
    k = pl.program_id(0)
    count = n // BLOCK

    @pl.when(k == 0)
    def _():
        raw = raw_ref[:, : width + EXTRA]
        pick = (lax.broadcasted_iota(jnp.int32, (8, EXTRA), 1) == 0).astype(jnp.bfloat16)
        place = dot(pick, raw[:, width:], NT)[0:1, :].astype(jnp.int32)
        target = lax.broadcasted_iota(jnp.int32, (1, n), 1) % count * BLOCK + place
        chosen = jnp.where(lax.broadcasted_iota(jnp.int32, (n, n), 0) == target, 1.0, 0.0).astype(jnp.bfloat16)
        sorted_ref[...] = dot(chosen, raw, NN).astype(jnp.bfloat16)
        gram = dot(sorted_ref[:, :width], sorted_ref[:, :width], NT)
        ridge = ATOM_RIDGE * sorted_ref[:, lane(width, PIVOT_ATOMS)].astype(jnp.float32)
        hit = lax.broadcasted_iota(jnp.int32, (n, n), 0) == lax.broadcasted_iota(jnp.int32, (n, n), 1)
        w_ref[...] = gram * gram + jnp.where(hit, ridge, 0.0)

    at = pl.multiple_of(k * BLOCK, BLOCK)
    rows_ref[...] = sorted_ref[pl.ds(at, BLOCK), :]
    mat_ref[...] = w_ref[pl.ds(at, BLOCK), pl.ds(at, BLOCK)]
    eliminate(mat_ref, inv_ref, out_ref)

    for step in range(count):

        @pl.when(k == step)
        def _(step=step):
            here, after = slice(step * BLOCK, (step + 1) * BLOCK), slice((step + 1) * BLOCK, n)
            inv = split(out_ref[...])
            high_ref[:, here], low_ref[:, here] = inv
            if step:
                left = split(dot(by_lhs(inv), by_rhs(split(w_ref[here, : step * BLOCK]), 0), NN))
                high_ref[:, : step * BLOCK], low_ref[:, : step * BLOCK] = left
            if step + 1 < count:
                zeros = jnp.zeros((BLOCK, n - (step + 1) * BLOCK), jnp.bfloat16)
                high_ref[:, after], low_ref[:, after] = zeros, zeros
                lower = split(dot(by_lhs(split(w_ref[after, here])), by_rhs(inv, 1), NT))
                lhs, rhs = by_lhs(lower), by_rhs(lower, 1)
                for first in range((step + 1) * BLOCK, n, 2 * BLOCK):
                    last = min(first + 2 * BLOCK, n)
                    skip = first - (step + 1) * BLOCK
                    w_ref[first:, first:last] = w_ref[first:, first:last] - dot(lhs[skip:], rhs[skip : skip + last - first], NT)
                w_ref[after, here] = -dot(lhs, by_rhs(inv, 0), NN)
                if step:
                    w_ref[after, : step * BLOCK] = w_ref[after, : step * BLOCK] - dot(lhs, by_rhs(left, 0), NN)


def by_lhs(parts):
    high, low = parts
    return jnp.concatenate([high, high, low], axis=1)


def by_rhs(parts, axis):
    high, low = parts
    return jnp.concatenate([high, low, high], axis=axis)


def lane(width, index):
    return slice(width + index, width + index + 1)


def pivot_factor(raw, width):
    n, packed = raw.shape[0], width + EXTRA
    return pl.pallas_call(
        functools.partial(pivot_kernel, n, width),
        grid=(n // BLOCK,),
        out_shape=tuple(pltpu.HBM((n, size), jnp.bfloat16) for size in (packed, n, n)),
        in_specs=[pl.BlockSpec(raw.shape, lambda k: (0, 0), pipeline_mode=pl.Buffered(1))],
        out_specs=tuple(pl.BlockSpec((BLOCK, size), lambda k: (k, 0)) for size in (packed, n, n)),
        scratch_shapes=[pltpu.VMEM((n, packed), jnp.bfloat16), pltpu.VMEM((n, n), jnp.float32)]
        + [pltpu.VMEM((BLOCK, BLOCK), jnp.float32)] * 3,
        compiler_params=pltpu.CompilerParams(vmem_limit_bytes=40 << 20),
        name="pivot_factor",
    )(pltpu.with_memory_space_constraint(raw, pltpu.HBM))


def pivot_stored(index, grid_rows, row_group):
    panel = index // NB
    return panel % grid_rows * row_group + panel // grid_rows * NB + index % NB


def final_kernel(
    grid_rows, grid_cols, row_group, width, row_tiles,
    at_ref, rows_ref, pivots_ref, high_ref, low_ref, col_ref, panel_ref, out_ref, w_ref, c_ref,
):
    step = pl.program_id(0)
    n = pivots_ref.shape[0]

    @pl.when(step < row_tiles)
    def _():
        tile = panel_ref.shape[0]
        at = pl.ds(pl.multiple_of(step * tile, tile), tile)
        gram = dot(rows_ref[at, :width], pivots_ref[:, :width], NT)
        ridge = ATOM_RIDGE * rows_ref[at, lane(width, OWN_ATOMS)].astype(jnp.float32)
        local = lax.broadcasted_iota(jnp.int32, (tile, n), 0) + step * tile
        pivot = lax.broadcasted_iota(jnp.int32, (tile, n), 1)
        stored = local + at_ref[0] * row_group
        cov = split(gram * gram + jnp.where(stored == pivot_stored(pivot, grid_rows, row_group), ridge, 0.0))
        row_tile = local // NB * grid_rows + at_ref[0]
        parts = []
        for p in range(n // PIECE):
            here, upto = slice(p * PIECE, (p + 1) * PIECE), slice(0, (p + 1) * PIECE)
            part = dot(by_lhs([x[:, upto] for x in cov]), by_rhs((high_ref[here, upto], low_ref[here, upto]), 1), NT)
            part = jnp.where(row_tile[:, here] >= p * PIECE // NB, part, 0.0)
            panel_ref[:, here] = part
            parts.append(split(part))
        panel = [jnp.concatenate([x[i] for x in parts], axis=1) for i in range(2)]
        for p in range(n // PIECE):
            here, since = slice(p * PIECE, (p + 1) * PIECE), slice(p * PIECE, n)
            part = dot(by_lhs([x[:, since] for x in panel]), by_rhs((high_ref[since, here], low_ref[since, here]), 0), NN)
            high, low = split(part)
            w_ref[at, here] = high
            w_ref[at, n + p * PIECE : n + (p + 1) * PIECE] = high
            w_ref[at, 2 * n + p * PIECE : 2 * n + (p + 1) * PIECE] = low

    @pl.when(step >= row_tiles)
    def _():
        total, tile = out_ref.shape
        col = lax.broadcasted_iota(jnp.int32, (n, tile), 1) + (step - row_tiles) * tile
        col_stored = (col // row_group * grid_cols + at_ref[1]) * row_group + col % row_group
        row = lax.broadcasted_iota(jnp.int32, (n, tile), 0)
        gram = dot(pivots_ref[:, :width], col_ref[...], NT)
        ridge = ATOM_RIDGE * pivots_ref[:, lane(width, PIVOT_ATOMS)].astype(jnp.float32)
        hit = pivot_stored(row, grid_rows, row_group) == col_stored
        high, low = split(gram * gram + jnp.where(hit, ridge, 0.0))
        c_ref[:n], c_ref[n : 2 * n], c_ref[2 * n :] = high, low, high
        gram = dot(rows_ref[:, :width], col_ref[...], NT)
        ridge = ATOM_RIDGE * rows_ref[:, lane(width, OWN_ATOMS)].astype(jnp.float32)
        hit = row[:total] + at_ref[0] * row_group == col_stored[:total]
        out_ref[...] = gram * gram + jnp.where(hit, ridge, 0.0) - dot(w_ref[...], c_ref[...], NN)


def final(at, rows, pivots, high, low, cols, grid_rows, grid_cols, row_group, width, row_tile=512, col_tile=512):
    count, total, n = rows.shape[0], cols.shape[0], pivots.shape[0]
    row_tiles = count // row_tile
    whole = lambda x: pl.BlockSpec(x.shape, lambda i, at: (0, 0), pipeline_mode=pl.Buffered(1))
    return pl.pallas_call(
        functools.partial(final_kernel, grid_rows, grid_cols, row_group, width, row_tiles),
        grid_spec=pltpu.PrefetchScalarGridSpec(
            num_scalar_prefetch=1,
            grid=(row_tiles + total // col_tile,),
            in_specs=[whole(rows), whole(pivots), whole(high), whole(low)]
            + [pl.BlockSpec((col_tile, width), lambda i, at: (jnp.maximum(i - row_tiles, 0), 0))],
            out_specs=(
                pl.BlockSpec((row_tile, n), lambda i, at: (jnp.minimum(i, row_tiles - 1), 0)),
                pl.BlockSpec((count, col_tile), lambda i, at: (0, jnp.maximum(i - row_tiles, 0))),
            ),
            scratch_shapes=[pltpu.VMEM((count, 3 * n), jnp.bfloat16), pltpu.VMEM((3 * n, col_tile), jnp.bfloat16)],
        ),
        out_shape=(
            jax.ShapeDtypeStruct((count, n), jnp.float32),
            jax.ShapeDtypeStruct((count, total), jnp.float32),
        ),
        compiler_params=pltpu.CompilerParams(vmem_limit_bytes=52 << 20),
        name="final",
    )(at, pltpu.with_memory_space_constraint(rows, pltpu.HBM), pivots, high, low, cols)


def in_block_order(rows, place):
    pick = lax.broadcasted_iota(jnp.int32, (rows.shape[0], rows.shape[0]), 0) == place.astype(jnp.int32)[None, :]
    return dot(pick.astype(jnp.bfloat16), rows, NN).astype(jnp.bfloat16)


def body(spectra, projection, kernel_slot, env_image, image_atoms):
    grid_rows = lax.axis_size("row")
    grid_cols = lax.axis_size("col")
    devices = grid_rows * grid_cols
    per_device = spectra.shape[0]
    width = projection.shape[1]
    row_group = per_device * grid_cols
    both = ("row", "col")
    projected = jnp.dot(spectra, projection, preferred_element_type=jnp.float32)
    factor = lax.rsqrt(
        jnp.mean(projected * projected, axis=1, keepdims=True) + NORM_EPS
    ) * width ** (-0.5)
    unit_rows = (projected * factor).astype(jnp.bfloat16)

    images = jnp.arange(image_atoms.shape[0], dtype=jnp.int32)
    atoms = jnp.sum(jnp.where(env_image[:, None] == images[None, :], image_atoms[None, :], 0), axis=1)
    extra_lane = jnp.arange(EXTRA, dtype=jnp.int32)[None, :]
    extra = jnp.where(extra_lane == 0, (kernel_slot % per_device)[:, None], atoms[:, None])
    packed = jnp.concatenate([unit_rows, extra.astype(jnp.bfloat16)], axis=1)

    block = kernel_slot // per_device
    blocks = jnp.arange(devices, dtype=jnp.int32)
    tile_blocks = NB // per_device
    group_blocks = row_group // per_device
    pivot_block = []
    for panel_index in range(PANELS):
        first = panel_index % grid_rows * group_blocks + panel_index // grid_rows * tile_blocks
        pivot_block += [first + i for i in range(tile_blocks)]
    pivot_block = jnp.stack([jnp.int32(i) for i in pivot_block])
    pivot_rows = dot((pivot_block[:, None] == block[None, :]).astype(jnp.bfloat16), packed, NN).astype(jnp.bfloat16)
    count = pivot_rows.shape[0]
    dest_row, dest_col = blocks // grid_cols, blocks % grid_cols
    turned_block = (dest_col + grid_cols * (dest_row // grid_cols)) * grid_cols + dest_row % grid_cols
    turned = dot((turned_block[:, None] == block[None, :]).astype(jnp.bfloat16), packed, NN).astype(jnp.bfloat16)
    own = dot((blocks[:, None] == block[None, :]).astype(jnp.bfloat16), packed, NN).astype(jnp.bfloat16)
    pair = jnp.concatenate([turned[:, :width], own[:, :width]], axis=1).reshape(devices, count, -1)
    spare = jnp.arange(EXTRA)
    spare = jnp.where(spare == 2, turned[:, width, None], jnp.where(spare == 3, own[:, width, None], own[:, width + 1, None]))
    head = jnp.broadcast_to(pivot_rows[None, :, :width], (devices, count, width))
    middle = jnp.where(jnp.arange(EXTRA) < 2, pivot_rows[None, :, width:], spare[:, None, :])
    parcel = jnp.concatenate([head, middle, pair], axis=2)

    parcel = lax.all_to_all(parcel, both, split_axis=0, concat_axis=0, tiled=True)
    pair = parcel[:, :, width + EXTRA :].reshape(per_device, 2 * width)
    places = parcel[:, 0, width : width + EXTRA]
    turned = in_block_order(pair[:, :width], places[:, 2])
    own = in_block_order(jnp.concatenate([pair[:, width:], places], axis=1), places[:, 3])
    col_rows = lax.all_gather(turned, "row", axis=0, tiled=True)
    row_rows = jnp.broadcast_to(own[None], (grid_cols,) + own.shape)
    row_rows = lax.all_to_all(row_rows, "col", split_axis=0, concat_axis=0)
    row_rows = row_rows.reshape(row_group, -1)
    pivots, high, low = pivot_factor(parcel.reshape(-1, parcel.shape[-1]), width)

    at = jnp.stack([lax.axis_index("row"), lax.axis_index("col")]).astype(jnp.int32)
    return final(at, row_rows, pivots, high, low, col_rows, grid_rows, grid_cols, row_group, width)


def solution(mesh):
    in_specs = (P(("row", "col"), None), P(), P(("row", "col")), P(("row", "col")), P())
    out_specs = (P("row", None), P("row", "col"))
    return jax.shard_map(body, mesh=mesh, in_specs=in_specs, out_specs=out_specs, check_vma=False)
```

```python
import functools

import jax
import jax.numpy as jnp
from jax import lax
from jax.experimental import pallas as pl
from jax.experimental.pallas import tpu as pltpu
from jax.sharding import PartitionSpec as P


NB = 512
PANELS = 2
ATOM_RIDGE = 0.02
NORM_EPS = 1e-06
EXTRA = 128
PIVOT_ATOMS = 1
OWN_ATOMS = 4
BLOCK = 128
PIECE = 256
NN = ((1,), (0,))
NT = ((1,), (1,))


def split(a):
    high = a.astype(jnp.bfloat16)
    return high, (a - high.astype(jnp.float32)).astype(jnp.bfloat16)


def dot(a, b, dims):
    return lax.dot_general(a, b, (dims, ((), ())), preferred_element_type=jnp.float32)


def eliminate(mat_ref, inv_ref, out_ref):
    sub = lax.broadcasted_iota(jnp.int32, (8, BLOCK), 0)
    column = lax.broadcasted_iota(jnp.int32, (8, BLOCK), 1)
    count = BLOCK // 8

    def wide(value):
        return jnp.broadcast_to(value, (8, BLOCK))

    for v in range(count):
        inv_ref[8 * v : 8 * v + 8, :] = jnp.where(column == sub + 8 * v, 1.0, 0.0)
    for v in range(count):
        mat, inv = mat_ref[8 * v : 8 * v + 8, :], inv_ref[8 * v : 8 * v + 8, :]
        cols = [wide(mat[:, 8 * v + k : 8 * v + k + 1]) for k in range(8)]
        done = inv
        for s in range(0, 8, 2):
            c0, c1 = cols[s], cols[s + 1]
            a, b, c = wide(c0[s : s + 1]), wide(c0[s + 1 : s + 2]), wide(c1[s + 1 : s + 2])
            det = a * c - b * b
            r = 1.0 / det
            c0, c1 = c0 - jnp.where(sub == s, 1.0, 0.0), c1 - jnp.where(sub == s + 1, 1.0, 0.0)
            u, w = c0 * c - c1 * b, c1 * a - c0 * b

            def apply(x):
                return x - (u * wide(x[s : s + 1]) + w * wide(x[s + 1 : s + 2])) * r

            for k in range(s + 2, 8):
                cols[k] = apply(cols[k])
            i0, i1 = wide(inv[s : s + 1]), wide(inv[s + 1 : s + 2])
            ra = lax.rsqrt(a)
            done = jnp.where(sub == s, i0 * ra, jnp.where(sub == s + 1, (a * i1 - b * i0) * (ra * lax.rsqrt(det)), done))
            mat, inv = apply(mat), apply(inv)
        out_ref[8 * v : 8 * v + 8, :] = done
        mats = [wide(mat[k : k + 1]) for k in range(8)]
        invs = [wide(inv[k : k + 1]) for k in range(8)]
        for i in range(v + 1, count):
            at = slice(8 * i, 8 * i + 8)
            x = mat_ref[at, :]
            parts = [wide(x[:, 8 * v + k : 8 * v + k + 1]) for k in range(8)]
            mat_ref[at, :] = x - tree_sum([p * m for p, m in zip(parts, mats)])
            inv_ref[at, :] = inv_ref[at, :] - tree_sum([p * m for p, m in zip(parts, invs)])


def tree_sum(values):
    while len(values) > 1:
        values = [values[i] + values[i + 1] for i in range(0, len(values), 2)]
    return values[0]


def pivot_kernel(n, width, core_ref, own_ref, other_ref, rows_ref, high_ref, low_ref, sorted_ref, w_ref, mat_ref, inv_ref, out_ref):
    k = pl.program_id(0)
    count = n // BLOCK

    @pl.when(k == 0)
    def _():
        half, share = width // 2, n // 2
        pick = (lax.broadcasted_iota(jnp.int32, (8, EXTRA), 1) == 0).astype(jnp.bfloat16)
        for source, raw_ref in ((core_ref[0], own_ref), (1 - core_ref[0], other_ref)):
            here = pl.ds(pl.multiple_of(source * share, share), share)
            raw = raw_ref[:, : half + EXTRA]
            place = dot(pick, raw[:, half:], NT)[0:1, :].astype(jnp.int32)
            line = lax.broadcasted_iota(jnp.int32, (1, n), 1) % count
            target = line // 2 * BLOCK + place
            out = lax.broadcasted_iota(jnp.int32, (share, n), 0)
            left = jnp.where(out == jnp.where(line % 2 == 0, target, -1), 1.0, 0.0).astype(jnp.bfloat16)
            left = dot(left, raw, NN).astype(jnp.bfloat16)
            right = jnp.where(out == jnp.where(line % 2 == 1, target, -1), 1.0, 0.0).astype(jnp.bfloat16)
            sorted_ref[here, :half] = left[:, :half]
            sorted_ref[here, half:width] = dot(right, raw[:, :half], NN).astype(jnp.bfloat16)
            sorted_ref[here, width:] = left[:, half:]
        gram = dot(sorted_ref[:, :width], sorted_ref[:, :width], NT)
        ridge = ATOM_RIDGE * sorted_ref[:, lane(width, PIVOT_ATOMS)].astype(jnp.float32)
        hit = lax.broadcasted_iota(jnp.int32, (n, n), 0) == lax.broadcasted_iota(jnp.int32, (n, n), 1)
        w_ref[...] = gram * gram + jnp.where(hit, ridge, 0.0)

    at = pl.multiple_of(k * BLOCK, BLOCK)
    rows_ref[...] = sorted_ref[pl.ds(at, BLOCK), :]
    mat_ref[...] = w_ref[pl.ds(at, BLOCK), pl.ds(at, BLOCK)]
    eliminate(mat_ref, inv_ref, out_ref)

    for step in range(count):

        @pl.when(k == step)
        def _(step=step):
            here, after = slice(step * BLOCK, (step + 1) * BLOCK), slice((step + 1) * BLOCK, n)
            inv = split(out_ref[...])
            high_ref[:, here], low_ref[:, here] = inv
            if step:
                left = split(dot(by_lhs(inv), by_rhs(split(w_ref[here, : step * BLOCK]), 0), NN))
                high_ref[:, : step * BLOCK], low_ref[:, : step * BLOCK] = left
            if step + 1 < count:
                zeros = jnp.zeros((BLOCK, n - (step + 1) * BLOCK), jnp.bfloat16)
                high_ref[:, after], low_ref[:, after] = zeros, zeros
                lower = split(dot(by_lhs(split(w_ref[after, here])), by_rhs(inv, 1), NT))
                lhs, rhs = by_lhs(lower), by_rhs(lower, 1)
                for first in range((step + 1) * BLOCK, n, 2 * BLOCK):
                    last = min(first + 2 * BLOCK, n)
                    skip = first - (step + 1) * BLOCK
                    w_ref[first:, first:last] = w_ref[first:, first:last] - dot(lhs[skip:], rhs[skip : skip + last - first], NT)
                w_ref[after, here] = -dot(lhs, by_rhs(inv, 0), NN)
                if step:
                    w_ref[after, : step * BLOCK] = w_ref[after, : step * BLOCK] - dot(lhs, by_rhs(left, 0), NN)


def by_lhs(parts):
    high, low = parts
    return jnp.concatenate([high, high, low], axis=1)


def by_rhs(parts, axis):
    high, low = parts
    return jnp.concatenate([high, low, high], axis=axis)


def lane(width, index):
    return slice(width + index, width + index + 1)


def pivot_factor(core, own, other, width):
    n, packed = own.shape[0], width + EXTRA
    raw = pl.BlockSpec(own.shape, lambda k, core: (0, 0), pipeline_mode=pl.Buffered(1))
    return pl.pallas_call(
        functools.partial(pivot_kernel, n, width),
        grid_spec=pltpu.PrefetchScalarGridSpec(
            num_scalar_prefetch=1,
            grid=(n // BLOCK,),
            in_specs=[raw, raw],
            out_specs=tuple(pl.BlockSpec((BLOCK, size), lambda k, core: (k, 0)) for size in (packed, n, n)),
            scratch_shapes=[pltpu.VMEM((n, packed), jnp.bfloat16), pltpu.VMEM((n, n), jnp.float32)]
            + [pltpu.VMEM((BLOCK, BLOCK), jnp.float32)] * 3,
        ),
        out_shape=tuple(pltpu.HBM((n, size), jnp.bfloat16) for size in (packed, n, n)),
        compiler_params=pltpu.CompilerParams(vmem_limit_bytes=40 << 20),
        name="pivot_factor",
    )(core, pltpu.with_memory_space_constraint(own, pltpu.HBM), pltpu.with_memory_space_constraint(other, pltpu.HBM))


def pivot_stored(index, grid_rows, row_group):
    panel = index // NB
    return panel % grid_rows * row_group + panel // grid_rows * NB + index % NB


def final_kernel(
    grid_rows, grid_cols, row_group, width, row_tiles,
    at_ref, rows_ref, pivots_ref, high_ref, low_ref, col_ref, panel_ref, out_ref, w_ref, c_ref,
):
    step = pl.program_id(0)
    n = pivots_ref.shape[0]

    @pl.when(step < row_tiles)
    def _():
        tile = panel_ref.shape[0]
        at = pl.ds(pl.multiple_of(step * tile, tile), tile)
        gram = dot(rows_ref[at, :width], pivots_ref[:, :width], NT)
        ridge = ATOM_RIDGE * rows_ref[at, lane(width, OWN_ATOMS)].astype(jnp.float32)
        local = lax.broadcasted_iota(jnp.int32, (tile, n), 0) + step * tile
        pivot = lax.broadcasted_iota(jnp.int32, (tile, n), 1)
        stored = local + at_ref[0] * row_group
        cov = split(gram * gram + jnp.where(stored == pivot_stored(pivot, grid_rows, row_group), ridge, 0.0))
        row_tile = local // NB * grid_rows + at_ref[0]
        parts = []
        for p in range(n // PIECE):
            here, upto = slice(p * PIECE, (p + 1) * PIECE), slice(0, (p + 1) * PIECE)
            part = dot(by_lhs([x[:, upto] for x in cov]), by_rhs((high_ref[here, upto], low_ref[here, upto]), 1), NT)
            part = jnp.where(row_tile[:, here] >= p * PIECE // NB, part, 0.0)
            panel_ref[:, here] = part
            parts.append(split(part))
        panel = [jnp.concatenate([x[i] for x in parts], axis=1) for i in range(2)]
        for p in range(n // PIECE):
            here, since = slice(p * PIECE, (p + 1) * PIECE), slice(p * PIECE, n)
            part = dot(by_lhs([x[:, since] for x in panel]), by_rhs((high_ref[since, here], low_ref[since, here]), 0), NN)
            high, low = split(part)
            w_ref[at, here] = high
            w_ref[at, n + p * PIECE : n + (p + 1) * PIECE] = high
            w_ref[at, 2 * n + p * PIECE : 2 * n + (p + 1) * PIECE] = low

    @pl.when(step >= row_tiles)
    def _():
        total, tile = out_ref.shape
        col = lax.broadcasted_iota(jnp.int32, (n, tile), 1) + (step - row_tiles) * tile
        col_stored = (col // row_group * grid_cols + at_ref[1]) * row_group + col % row_group
        row = lax.broadcasted_iota(jnp.int32, (n, tile), 0)
        gram = dot(pivots_ref[:, :width], col_ref[...], NT)
        ridge = ATOM_RIDGE * pivots_ref[:, lane(width, PIVOT_ATOMS)].astype(jnp.float32)
        hit = pivot_stored(row, grid_rows, row_group) == col_stored
        high, low = split(gram * gram + jnp.where(hit, ridge, 0.0))
        c_ref[:n], c_ref[n : 2 * n], c_ref[2 * n :] = high, low, high
        gram = dot(rows_ref[:, :width], col_ref[...], NT)
        ridge = ATOM_RIDGE * rows_ref[:, lane(width, OWN_ATOMS)].astype(jnp.float32)
        hit = row[:total] + at_ref[0] * row_group == col_stored[:total]
        out_ref[...] = gram * gram + jnp.where(hit, ridge, 0.0) - dot(w_ref[...], c_ref[...], NN)


def final(at, rows, pivots, high, low, cols, grid_rows, grid_cols, row_group, width, row_tile=512, col_tile=512):
    count, total, n = rows.shape[0], cols.shape[0], pivots.shape[0]
    row_tiles = count // row_tile
    whole = lambda x: pl.BlockSpec(x.shape, lambda i, at: (0, 0), pipeline_mode=pl.Buffered(1))
    return pl.pallas_call(
        functools.partial(final_kernel, grid_rows, grid_cols, row_group, width, row_tiles),
        grid_spec=pltpu.PrefetchScalarGridSpec(
            num_scalar_prefetch=1,
            grid=(row_tiles + total // col_tile,),
            in_specs=[whole(rows), whole(pivots), whole(high), whole(low)]
            + [pl.BlockSpec((col_tile, width), lambda i, at: (jnp.maximum(i - row_tiles, 0), 0))],
            out_specs=(
                pl.BlockSpec((row_tile, n), lambda i, at: (jnp.minimum(i, row_tiles - 1), 0)),
                pl.BlockSpec((count, col_tile), lambda i, at: (0, jnp.maximum(i - row_tiles, 0))),
            ),
            scratch_shapes=[pltpu.VMEM((count, 3 * n), jnp.bfloat16), pltpu.VMEM((3 * n, col_tile), jnp.bfloat16)],
        ),
        out_shape=(
            jax.ShapeDtypeStruct((count, n), jnp.float32),
            jax.ShapeDtypeStruct((count, total), jnp.float32),
        ),
        compiler_params=pltpu.CompilerParams(vmem_limit_bytes=52 << 20),
        name="final",
    )(at, pltpu.with_memory_space_constraint(rows, pltpu.HBM), pivots, high, low, cols)


def in_block_order(rows, place):
    pick = lax.broadcasted_iota(jnp.int32, (rows.shape[0], rows.shape[0]), 0) == place.astype(jnp.int32)[None, :]
    return dot(pick.astype(jnp.bfloat16), rows, NN).astype(jnp.bfloat16)


def body(spectra, projection, kernel_slot, env_image, image_atoms):
    grid_rows = lax.axis_size("row")
    grid_cols = lax.axis_size("col")
    devices = grid_rows * grid_cols
    per_device = spectra.shape[0]
    width = projection.shape[1]
    row_group = per_device * grid_cols
    both = ("row", "col")
    projected = jnp.dot(spectra, projection, preferred_element_type=jnp.float32)
    factor = lax.rsqrt(
        jnp.mean(projected * projected, axis=1, keepdims=True) + NORM_EPS
    ) * width ** (-0.5)
    unit_rows = (projected * factor).astype(jnp.bfloat16)

    images = jnp.arange(image_atoms.shape[0], dtype=jnp.int32)
    atoms = jnp.sum(jnp.where(env_image[:, None] == images[None, :], image_atoms[None, :], 0), axis=1)
    extra_lane = jnp.arange(EXTRA, dtype=jnp.int32)[None, :]
    extra = jnp.where(extra_lane == 0, (kernel_slot % per_device)[:, None], atoms[:, None])
    packed = jnp.concatenate([unit_rows, extra.astype(jnp.bfloat16)], axis=1)

    block = kernel_slot // per_device
    blocks = jnp.arange(devices, dtype=jnp.int32)
    tile_blocks = NB // per_device
    group_blocks = row_group // per_device
    pivot_block = []
    for panel_index in range(PANELS):
        first = panel_index % grid_rows * group_blocks + panel_index // grid_rows * tile_blocks
        pivot_block += [first + i for i in range(tile_blocks)]
    pivot_block = jnp.stack([jnp.int32(i) for i in pivot_block])
    pivot_rows = dot((pivot_block[:, None] == block[None, :]).astype(jnp.bfloat16), packed, NN).astype(jnp.bfloat16)
    count = pivot_rows.shape[0]
    dest_row, dest_col = blocks // grid_cols, blocks % grid_cols
    turned_block = (dest_col + grid_cols * (dest_row // grid_cols)) * grid_cols + dest_row % grid_cols
    turned = dot((turned_block[:, None] == block[None, :]).astype(jnp.bfloat16), packed, NN).astype(jnp.bfloat16)
    own = dot((blocks[:, None] == block[None, :]).astype(jnp.bfloat16), packed, NN).astype(jnp.bfloat16)
    half = width // 2
    heads = pivot_rows[:, :width].reshape(2, count, half)
    extras = jnp.repeat(pivot_rows[:, width:], 2, axis=0).reshape(2, count, EXTRA)
    core = (dest_col % 2)[:, None, None]
    pair = jnp.concatenate([turned[:, :width], own[:, :width]], axis=1).reshape(devices, count, -1)
    spare = jnp.arange(EXTRA)
    spare = jnp.where(spare == 2, turned[:, width, None], jnp.where(spare == 3, own[:, width, None], own[:, width + 1, None]))
    head = jnp.where(core == 0, heads[None, 0], heads[None, 1])
    middle = jnp.where(core == 0, extras[None, 0], extras[None, 1])
    middle = jnp.where(jnp.arange(EXTRA) < 2, middle, spare[:, None, :])
    parcel = jnp.concatenate([head, middle, pair], axis=2)

    parcel = lax.all_to_all(parcel, both, split_axis=0, concat_axis=0, tiled=True)
    lines = parcel.reshape(devices * count, -1)
    partner = lax.ppermute(lines, "col", [(i, i + 1 - i % 2 * 2) for i in range(grid_cols)])
    pair = parcel[:, :, half + EXTRA :].reshape(per_device, 2 * width)
    places = parcel[:, 0, half : half + EXTRA]
    turned = in_block_order(pair[:, :width], places[:, 2])
    own = in_block_order(jnp.concatenate([pair[:, width:], places], axis=1), places[:, 3])
    col_rows = lax.all_gather(turned, "row", axis=0, tiled=True)
    row_rows = jnp.broadcast_to(own[None], (grid_cols,) + own.shape)
    row_rows = lax.all_to_all(row_rows, "col", split_axis=0, concat_axis=0)
    row_rows = row_rows.reshape(row_group, -1)
    core = (lax.axis_index("col") % 2).astype(jnp.int32)[None]
    pivots, high, low = pivot_factor(core, lines, partner, width)

    at = jnp.stack([lax.axis_index("row"), lax.axis_index("col")]).astype(jnp.int32)
    return final(at, row_rows, pivots, high, low, col_rows, grid_rows, grid_cols, row_group, width)


def solution(mesh):
    in_specs = (P(("row", "col"), None), P(), P(("row", "col")), P(("row", "col")), P())
    out_specs = (P("row", None), P("row", "col"))
    return jax.shard_map(body, mesh=mesh, in_specs=in_specs, out_specs=out_specs, check_vma=False)
```

```python
import functools

import jax
import jax.numpy as jnp
from jax import lax
from jax.experimental import pallas as pl
from jax.experimental.pallas import tpu as pltpu
from jax.sharding import PartitionSpec as P


NB = 512
PANELS = 2
ATOM_RIDGE = 0.02
NORM_EPS = 1e-06
EXTRA = 128
PIVOT_ATOMS = 1
OWN_ATOMS = 4
BLOCK = 128
PIECE = 256
NN = ((1,), (0,))
NT = ((1,), (1,))


def split(a):
    high = a.astype(jnp.bfloat16)
    return high, (a - high.astype(jnp.float32)).astype(jnp.bfloat16)


def dot(a, b, dims):
    return lax.dot_general(a, b, (dims, ((), ())), preferred_element_type=jnp.float32)


def eliminate(mat_ref, inv_ref, out_ref):
    sub = lax.broadcasted_iota(jnp.int32, (8, BLOCK), 0)
    column = lax.broadcasted_iota(jnp.int32, (8, BLOCK), 1)
    count = BLOCK // 8

    def wide(value):
        return jnp.broadcast_to(value, (8, BLOCK))

    for v in range(count):
        inv_ref[8 * v : 8 * v + 8, :] = jnp.where(column == sub + 8 * v, 1.0, 0.0)
    for v in range(count):
        mat, inv = mat_ref[8 * v : 8 * v + 8, :], inv_ref[8 * v : 8 * v + 8, :]
        cols = [wide(mat[:, 8 * v + k : 8 * v + k + 1]) for k in range(8)]
        done = inv
        for s in range(0, 8, 2):
            c0, c1 = cols[s], cols[s + 1]
            a, b, c = wide(c0[s : s + 1]), wide(c0[s + 1 : s + 2]), wide(c1[s + 1 : s + 2])
            det = a * c - b * b
            r = 1.0 / det
            c0, c1 = c0 - jnp.where(sub == s, 1.0, 0.0), c1 - jnp.where(sub == s + 1, 1.0, 0.0)
            u, w = c0 * c - c1 * b, c1 * a - c0 * b

            def apply(x):
                return x - (u * wide(x[s : s + 1]) + w * wide(x[s + 1 : s + 2])) * r

            for k in range(s + 2, 8):
                cols[k] = apply(cols[k])
            i0, i1 = wide(inv[s : s + 1]), wide(inv[s + 1 : s + 2])
            ra = lax.rsqrt(a)
            done = jnp.where(sub == s, i0 * ra, jnp.where(sub == s + 1, (a * i1 - b * i0) * (ra * lax.rsqrt(det)), done))
            mat, inv = apply(mat), apply(inv)
        out_ref[8 * v : 8 * v + 8, :] = done
        mats = [wide(mat[k : k + 1]) for k in range(8)]
        invs = [wide(inv[k : k + 1]) for k in range(8)]
        for i in range(v + 1, count):
            at = slice(8 * i, 8 * i + 8)
            x = mat_ref[at, :]
            parts = [wide(x[:, 8 * v + k : 8 * v + k + 1]) for k in range(8)]
            mat_ref[at, :] = x - tree_sum([p * m for p, m in zip(parts, mats)])
            inv_ref[at, :] = inv_ref[at, :] - tree_sum([p * m for p, m in zip(parts, invs)])


def tree_sum(values):
    while len(values) > 1:
        values = [values[i] + values[i + 1] for i in range(0, len(values), 2)]
    return values[0]


def pivot_kernel(n, width, core_ref, own_ref, other_ref, rows_ref, high_ref, low_ref, sorted_ref, w_ref, mat_ref, inv_ref, out_ref):
    k = pl.program_id(0)
    count = n // BLOCK

    @pl.when(k == 0)
    def _():
        half, share = width // 2, n // 2
        pick = (lax.broadcasted_iota(jnp.int32, (8, EXTRA), 1) == 0).astype(jnp.bfloat16)
        for source, raw_ref in ((core_ref[0], own_ref), (1 - core_ref[0], other_ref)):
            here = pl.ds(pl.multiple_of(source * share, share), share)
            raw = raw_ref[...]
            place = dot(pick, raw[:, half:], NT)[0:1, :].astype(jnp.int32)
            line = lax.broadcasted_iota(jnp.int32, (1, n), 1) % count
            target = line // 2 * BLOCK + place
            out = lax.broadcasted_iota(jnp.int32, (share, n), 0)
            left = jnp.where(out == jnp.where(line % 2 == 0, target, -1), 1.0, 0.0).astype(jnp.bfloat16)
            left = dot(left, raw, NN).astype(jnp.bfloat16)
            right = jnp.where(out == jnp.where(line % 2 == 1, target, -1), 1.0, 0.0).astype(jnp.bfloat16)
            sorted_ref[here, :half] = left[:, :half]
            sorted_ref[here, half:width] = dot(right, raw[:, :half], NN).astype(jnp.bfloat16)
            sorted_ref[here, width:] = left[:, half:]
        for first in range(0, n, PIECE):
            here = slice(first, first + PIECE)
            gram = dot(sorted_ref[first:, :width], sorted_ref[here, :width], NT)
            ridge = ATOM_RIDGE * sorted_ref[first:, lane(width, PIVOT_ATOMS)].astype(jnp.float32)
            hit = lax.broadcasted_iota(jnp.int32, gram.shape, 0) == lax.broadcasted_iota(jnp.int32, gram.shape, 1)
            w_ref[first:, here] = gram * gram + jnp.where(hit, ridge, 0.0)

    at = pl.multiple_of(k * BLOCK, BLOCK)
    rows_ref[...] = sorted_ref[pl.ds(at, BLOCK), :]
    mat_ref[...] = w_ref[pl.ds(at, BLOCK), pl.ds(at, BLOCK)]
    eliminate(mat_ref, inv_ref, out_ref)

    for step in range(count):

        @pl.when(k == step)
        def _(step=step):
            here, after = slice(step * BLOCK, (step + 1) * BLOCK), slice((step + 1) * BLOCK, n)
            inv = split(out_ref[...])
            high_ref[:, here], low_ref[:, here] = inv
            if step:
                left = split(dot(by_lhs(inv), by_rhs(split(w_ref[here, : step * BLOCK]), 0), NN))
                high_ref[:, : step * BLOCK], low_ref[:, : step * BLOCK] = left
            if step + 1 < count:
                zeros = jnp.zeros((BLOCK, n - (step + 1) * BLOCK), jnp.bfloat16)
                high_ref[:, after], low_ref[:, after] = zeros, zeros
                lower = split(dot(by_lhs(split(w_ref[after, here])), by_rhs(inv, 1), NT))
                lhs, rhs = by_lhs(lower), by_rhs(lower, 1)
                for first in range((step + 1) * BLOCK, n, 2 * BLOCK):
                    last = min(first + 2 * BLOCK, n)
                    skip = first - (step + 1) * BLOCK
                    w_ref[first:, first:last] = w_ref[first:, first:last] - dot(lhs[skip:], rhs[skip : skip + last - first], NT)
                w_ref[after, here] = -dot(lhs, by_rhs(inv, 0), NN)
                if step:
                    w_ref[after, : step * BLOCK] = w_ref[after, : step * BLOCK] - dot(lhs, by_rhs(left, 0), NN)


def by_lhs(parts):
    high, low = parts
    return jnp.concatenate([high, high, low], axis=1)


def by_rhs(parts, axis):
    high, low = parts
    return jnp.concatenate([high, low, high], axis=axis)


def lane(width, index):
    return slice(width + index, width + index + 1)


def pivot_factor(core, own, other, width):
    n, packed = own.shape[0], width + EXTRA
    raw = pl.BlockSpec((n, width // 2 + EXTRA), lambda k, core: (0, 0), pipeline_mode=pl.Buffered(1))
    return pl.pallas_call(
        functools.partial(pivot_kernel, n, width),
        grid_spec=pltpu.PrefetchScalarGridSpec(
            num_scalar_prefetch=1,
            grid=(n // BLOCK,),
            in_specs=[raw, raw],
            out_specs=tuple(pl.BlockSpec((BLOCK, size), lambda k, core: (k, 0)) for size in (packed, n, n)),
            scratch_shapes=[pltpu.VMEM((n, packed), jnp.bfloat16), pltpu.VMEM((n, n), jnp.float32)]
            + [pltpu.VMEM((BLOCK, BLOCK), jnp.float32)] * 3,
        ),
        out_shape=tuple(pltpu.HBM((n, size), jnp.bfloat16) for size in (packed, n, n)),
        compiler_params=pltpu.CompilerParams(vmem_limit_bytes=40 << 20),
        name="pivot_factor",
    )(core, pltpu.with_memory_space_constraint(own, pltpu.HBM), pltpu.with_memory_space_constraint(other, pltpu.HBM))


def pivot_stored(index, grid_rows, row_group):
    panel = index // NB
    return panel % grid_rows * row_group + panel // grid_rows * NB + index % NB


def final_kernel(
    grid_rows, grid_cols, row_group, width, row_tiles,
    at_ref, rows_ref, pivots_ref, high_ref, low_ref, col_ref, panel_ref, out_ref, w_ref, c_ref,
):
    step = pl.program_id(0)
    n = pivots_ref.shape[0]

    @pl.when(step < row_tiles)
    def _():
        tile = panel_ref.shape[0]
        at = pl.ds(pl.multiple_of(step * tile, tile), tile)
        gram = dot(rows_ref[at, :width], pivots_ref[:, :width], NT)
        ridge = ATOM_RIDGE * rows_ref[at, lane(width, OWN_ATOMS)].astype(jnp.float32)
        local = lax.broadcasted_iota(jnp.int32, (tile, n), 0) + step * tile
        pivot = lax.broadcasted_iota(jnp.int32, (tile, n), 1)
        stored = local + at_ref[0] * row_group
        cov = split(gram * gram + jnp.where(stored == pivot_stored(pivot, grid_rows, row_group), ridge, 0.0))
        row_tile = local // NB * grid_rows + at_ref[0]
        parts = []
        for p in range(n // PIECE):
            here, upto = slice(p * PIECE, (p + 1) * PIECE), slice(0, (p + 1) * PIECE)
            part = dot(by_lhs([x[:, upto] for x in cov]), by_rhs((high_ref[here, upto], low_ref[here, upto]), 1), NT)
            part = jnp.where(row_tile[:, here] >= p * PIECE // NB, part, 0.0)
            panel_ref[:, here] = part
            parts.append(split(part))
        panel = [jnp.concatenate([x[i] for x in parts], axis=1) for i in range(2)]
        for p in range(n // PIECE):
            here, since = slice(p * PIECE, (p + 1) * PIECE), slice(p * PIECE, n)
            part = dot(by_lhs([x[:, since] for x in panel]), by_rhs((high_ref[since, here], low_ref[since, here]), 0), NN)
            high, low = split(part)
            w_ref[at, here] = high
            w_ref[at, n + p * PIECE : n + (p + 1) * PIECE] = high
            w_ref[at, 2 * n + p * PIECE : 2 * n + (p + 1) * PIECE] = low

    @pl.when(step >= row_tiles)
    def _():
        total, tile = out_ref.shape
        col = lax.broadcasted_iota(jnp.int32, (n, tile), 1) + (step - row_tiles) * tile
        col_stored = (col // row_group * grid_cols + at_ref[1]) * row_group + col % row_group
        row = lax.broadcasted_iota(jnp.int32, (n, tile), 0)
        gram = dot(pivots_ref[:, :width], col_ref[...], NT)
        ridge = ATOM_RIDGE * pivots_ref[:, lane(width, PIVOT_ATOMS)].astype(jnp.float32)
        hit = pivot_stored(row, grid_rows, row_group) == col_stored
        high, low = split(gram * gram + jnp.where(hit, ridge, 0.0))
        c_ref[:n], c_ref[n : 2 * n], c_ref[2 * n :] = high, low, high
        gram = dot(rows_ref[:, :width], col_ref[...], NT)
        ridge = ATOM_RIDGE * rows_ref[:, lane(width, OWN_ATOMS)].astype(jnp.float32)
        hit = row[:total] + at_ref[0] * row_group == col_stored[:total]
        out_ref[...] = gram * gram + jnp.where(hit, ridge, 0.0) - dot(w_ref[...], c_ref[...], NN)


def final(at, rows, pivots, high, low, cols, grid_rows, grid_cols, row_group, width, row_tile=512, col_tile=512):
    count, total, n = rows.shape[0], cols.shape[0], pivots.shape[0]
    row_tiles = count // row_tile
    whole = lambda x: pl.BlockSpec(x.shape, lambda i, at: (0, 0), pipeline_mode=pl.Buffered(1))
    return pl.pallas_call(
        functools.partial(final_kernel, grid_rows, grid_cols, row_group, width, row_tiles),
        grid_spec=pltpu.PrefetchScalarGridSpec(
            num_scalar_prefetch=1,
            grid=(row_tiles + total // col_tile,),
            in_specs=[whole(rows), whole(pivots), whole(high), whole(low)]
            + [pl.BlockSpec((col_tile, width), lambda i, at: (jnp.maximum(i - row_tiles, 0), 0))],
            out_specs=(
                pl.BlockSpec((row_tile, n), lambda i, at: (jnp.minimum(i, row_tiles - 1), 0)),
                pl.BlockSpec((count, col_tile), lambda i, at: (0, jnp.maximum(i - row_tiles, 0))),
            ),
            scratch_shapes=[pltpu.VMEM((count, 3 * n), jnp.bfloat16), pltpu.VMEM((3 * n, col_tile), jnp.bfloat16)],
        ),
        out_shape=(
            jax.ShapeDtypeStruct((count, n), jnp.float32),
            jax.ShapeDtypeStruct((count, total), jnp.float32),
        ),
        compiler_params=pltpu.CompilerParams(vmem_limit_bytes=52 << 20),
        name="final",
    )(at, pltpu.with_memory_space_constraint(rows, pltpu.HBM), pivots, high, low, cols)


def in_block_order(rows, place):
    pick = lax.broadcasted_iota(jnp.int32, (rows.shape[0], rows.shape[0]), 0) == place.astype(jnp.int32)[None, :]
    return dot(pick.astype(jnp.bfloat16), rows, NN).astype(jnp.bfloat16)


def body(spectra, projection, kernel_slot, env_image, image_atoms):
    grid_rows = lax.axis_size("row")
    grid_cols = lax.axis_size("col")
    devices = grid_rows * grid_cols
    per_device = spectra.shape[0]
    width = projection.shape[1]
    row_group = per_device * grid_cols
    both = ("row", "col")
    projected = jnp.dot(spectra, projection, preferred_element_type=jnp.float32)
    factor = lax.rsqrt(
        jnp.mean(projected * projected, axis=1, keepdims=True) + NORM_EPS
    ) * width ** (-0.5)
    unit_rows = (projected * factor).astype(jnp.bfloat16)

    images = jnp.arange(image_atoms.shape[0], dtype=jnp.int32)
    atoms = jnp.sum(jnp.where(env_image[:, None] == images[None, :], image_atoms[None, :], 0), axis=1)
    extra_lane = jnp.arange(EXTRA, dtype=jnp.int32)[None, :]
    extra = jnp.where(extra_lane == 0, (kernel_slot % per_device)[:, None], atoms[:, None])
    packed = jnp.concatenate([unit_rows, extra.astype(jnp.bfloat16)], axis=1)

    block = kernel_slot // per_device
    blocks = jnp.arange(devices, dtype=jnp.int32)
    tile_blocks = NB // per_device
    group_blocks = row_group // per_device
    pivot_block = []
    for panel_index in range(PANELS):
        first = panel_index % grid_rows * group_blocks + panel_index // grid_rows * tile_blocks
        pivot_block += [first + i for i in range(tile_blocks)]
    pivot_block = jnp.stack([jnp.int32(i) for i in pivot_block])
    pivot_rows = dot((pivot_block[:, None] == block[None, :]).astype(jnp.bfloat16), packed, NN).astype(jnp.bfloat16)
    count = pivot_rows.shape[0]
    dest_row, dest_col = blocks // grid_cols, blocks % grid_cols
    turned_block = (dest_col + grid_cols * (dest_row // grid_cols)) * grid_cols + dest_row % grid_cols
    turned = dot((turned_block[:, None] == block[None, :]).astype(jnp.bfloat16), packed, NN).astype(jnp.bfloat16)
    own = dot((blocks[:, None] == block[None, :]).astype(jnp.bfloat16), packed, NN).astype(jnp.bfloat16)
    half = width // 2
    heads = pivot_rows[:, :width].reshape(2, count, half)
    extras = jnp.repeat(pivot_rows[:, width:], 2, axis=0).reshape(2, count, EXTRA)
    core = (dest_col % 2)[:, None, None]
    pair = jnp.concatenate([turned[:, :width], own[:, :width]], axis=1).reshape(devices, count, -1)
    spare = jnp.arange(EXTRA)
    spare = jnp.where(spare == 2, turned[:, width, None], jnp.where(spare == 3, own[:, width, None], own[:, width + 1, None]))
    head = jnp.where(core == 0, heads[None, 0], heads[None, 1])
    middle = jnp.where(core == 0, extras[None, 0], extras[None, 1])
    middle = jnp.where(jnp.arange(EXTRA) < 2, middle, spare[:, None, :])
    parcel = jnp.concatenate([head, middle, pair], axis=2)

    parcel = lax.all_to_all(parcel, both, split_axis=0, concat_axis=0, tiled=True)
    lines = parcel.reshape(devices * count, -1)
    partner = lax.ppermute(lines, "col", [(i, i + 1 - i % 2 * 2) for i in range(grid_cols)])
    pair = parcel[:, :, half + EXTRA :].reshape(per_device, 2 * width)
    places = parcel[:, 0, half : half + EXTRA]
    turned = in_block_order(pair[:, :width], places[:, 2])
    own = in_block_order(jnp.concatenate([pair[:, width:], places], axis=1), places[:, 3])
    col_rows = lax.all_gather(turned, "row", axis=0, tiled=True)
    row_rows = jnp.broadcast_to(own[None], (grid_cols,) + own.shape)
    row_rows = lax.all_to_all(row_rows, "col", split_axis=0, concat_axis=0)
    row_rows = row_rows.reshape(row_group, -1)
    core = (lax.axis_index("col") % 2).astype(jnp.int32)[None]
    pivots, high, low = pivot_factor(core, lines, partner, width)

    at = jnp.stack([lax.axis_index("row"), lax.axis_index("col")]).astype(jnp.int32)
    return final(at, row_rows, pivots, high, low, col_rows, grid_rows, grid_cols, row_group, width)


def solution(mesh):
    in_specs = (P(("row", "col"), None), P(), P(("row", "col")), P(("row", "col")), P())
    out_specs = (P("row", None), P("row", "col"))
    return jax.shard_map(body, mesh=mesh, in_specs=in_specs, out_specs=out_specs, check_vma=False)
```
